32 devices in a mesh: groups: 2 (over y), markov: 4 (over z), storage: 2 (over x), sub: 2 (over core).
Axes of the slice: x: 2, y: 2, z: 4, core: 2. Of those that a mesh axis runs over, the one named last changes fastest.
Arguments:
- expected_cot: bfloat16 [8192, 2048], P(('groups', 'markov'), ('storage', 'sub')), parts along dimension 0, may hold values from -192 to 192
- value_next: bfloat16 [8192, 2048], P(('groups', 'markov'), ('storage', 'sub')), parts along dimension 0, may hold values from -0.0024414062 to 0.0024414062
- transition: bfloat16 [8192, 4096], P(('groups', 'storage', 'sub'), 'markov'), parts along dimension 0, may hold values from 6.1035156e-05 to 0.0009765625
- section: int32 [2], P('groups'), parts along dimension 0, may hold values from 0 to 51
Outputs:
- section_adjoint: float32 [8192, 2048], P(('groups', 'markov'), ('storage', 'sub')), parts along dimension 0
- transition_grad: float32 [8192, 4096], P(('groups', 'storage', 'sub'), 'markov'), parts along dimension 0
The draws below stay inside these ranges and needn't reach their ends.
There are 2 independent parts, one for each index of `groups`. The reference program is written for one: setup_inputs(seed, part) draws one part's arguments, and reference() takes and returns one part's arrays. A program takes and returns all parts, laid end to end along the dimension named above; each array names one. Nothing has to cross between parts.
All inputs are finite; a program needn't handle non-finite values.
Results may differ from the reference program's by a relative error of at most 0.0003.
Values may be sent and summed in bfloat16 or wider, within the bound.
A program may use at most 64 MiB of HBM per device.

```python
import math
import jax
import jax.numpy as jnp
from jax import lax

M = 4096
SECTIONS = 52
CELLS = 2048


def steps_of(own_key, shape, shards, smallest, top_value):
    def one(dim, shards_of):
        heights = jax.random.uniform(jax.random.fold_in(jax.random.fold_in(own_key, 6), dim), (shards_of,), jnp.float32, smallest / len(shards), top_value / len(shards))
        return jnp.repeat(jnp.exp(heights), shape[dim] // shards_of).reshape((-1,) + (1,) * (len(shape) - dim - 1))

    loudness = one(*shards[0])
    for cut in shards[1:]:
        loudness = loudness * one(*cut)
    return loudness


def scatter_about(key, extent, width, reach, split=(), held_as=jnp.bfloat16):
    drawn = width * jax.random.normal(key, extent, jnp.float32)
    if split:
        drawn = drawn * steps_of(key, extent, split, -0.22, 0.18)
    return jnp.clip(drawn, -reach, reach).astype(held_as)


def setup_inputs(seed: int = 0, part: int = 0) -> dict:
    keys = jax.random.split(jax.random.key(seed), 5)
    own_keys = jax.random.split(jax.random.fold_in(keys[4], part), 5)
    expected_cot = scatter_about(own_keys[0], (M, CELLS), 32.0, 192.0, ((0, 4), (1, 4)))
    value_next = scatter_about(own_keys[1], (M, CELLS), 0.0004, 0.0024414062, ((0, 4), (1, 4)))
    transition = jnp.clip(jnp.exp(math.log(0.0009765625) - 2.7725887 * jax.random.uniform(own_keys[2], (M, M), jnp.float32) ** steps_of(own_keys[2], (M, M), ((0, 4), (1, 4)), -0.2, 0.2)), 6.103515625e-05, 0.0009765625).astype(jnp.bfloat16)
    section = jax.random.randint(own_keys[3], (1,), 0, SECTIONS).astype(jnp.int32)
    return {"expected_cot": expected_cot, "value_next": value_next, "transition": transition, "section": section}


discount_rate = 0.97


def reference(expected_cot, value_next, transition, section):
    discount_factor = jnp.exp(section[0].astype(jnp.float32) * jnp.log(jnp.float32(discount_rate)))
    adjoint_sum = lax.dot_general(transition, expected_cot, (((0,), (0,)), ((), ())), preferred_element_type=jnp.float32)
    gradient_sum = lax.dot_general(expected_cot, value_next, (((1,), (1,)), ((), ())), preferred_element_type=jnp.float32)
    return discount_factor * adjoint_sum, discount_factor * gradient_sum
```

```python
import functools

import jax
import jax.numpy as jnp
from jax import lax
from jax.experimental import pallas as pl
from jax.experimental.pallas import tpu as pltpu
from jax.sharding import PartitionSpec as P

discount_rate = 0.97
MESH = pl.DeviceIdType.MESH
PIECES = 2
TILE = 256


def discount_of(section):
    return jnp.exp(section[0].astype(jnp.float32) * jnp.log(jnp.float32(discount_rate)))


def gathered(expected_cot, value_next, transition, section):
    discount_factor = discount_of(section)
    cotangent_all = lax.all_gather(expected_cot, "markov", axis=0, tiled=True)
    adjoint_sum = lax.dot_general(
        lax.all_gather(transition, ("storage", "sub"), axis=0, tiled=True),
        cotangent_all,
        (((0,), (0,)), ((), ())),
        preferred_element_type=jnp.float32,
    )
    own_states = lax.all_to_all(
        cotangent_all, ("storage", "sub"), split_axis=0, concat_axis=1, tiled=True
    )
    gathered_values = lax.all_gather(value_next, ("storage", "sub"), axis=1, tiled=True)
    gradient_sum = lax.dot_general(
        own_states, gathered_values, (((1,), (1,)), ((), ())), preferred_element_type=jnp.float32
    )
    return (discount_factor * adjoint_sum, discount_factor * gradient_sum)


def kernel(
    n_z, c_in, v_in, t_in, adj, grad, c_all, c_row, t_all, v_all,
    local_sem, z_recv, up_send, down_send, tx_send, tx_recv, vx_send, vx_recv,
    tf_send, tf_recv, vf_send, vf_recv, tp_send, tp_recv, vp_send, vp_recv,
    cp_send, cp_recv, row_send, row_recv, flow_send,
):
    g, m = lax.axis_index("groups"), lax.axis_index("markov")
    s, u = lax.axis_index("storage"), lax.axis_index("sub")
    far = 1 - s
    j, p = 2 * s + u, 2 * s + 1 - u
    o, q = 2 * far + u, 2 * far + 1 - u
    partner, across, crossed = (g, m, s, 1 - u), (g, m, far, u), (g, m, far, 1 - u)
    above, below = (g, lax.rem(m + 1, n_z), s, u), (g, lax.rem(m + n_z - 1, n_z), s, u)
    has_up, has_down = m < n_z - 1, m > 0

    def crossing_row(chip, z):
        return jnp.clip(z, 2 * chip, 2 * chip + 1)

    sent_row = crossing_row(far, m)
    sent_own = sent_row == m
    by_x = crossing_row(s, m) == j
    flow_up = (m >= j) & has_up & (crossing_row(s, m + 1) != j)
    flow_down = (m <= j) & has_down & (crossing_row(s, m - 1) != j)

    def rows(ref, piece, *lead):
        step = ref.shape[-2] // PIECES
        return ref.at[(*lead, pl.ds(piece * step, step))]

    def remote(src, dst, send, recv, to):
        return pltpu.make_async_remote_copy(
            src_ref=src, dst_ref=dst, send_sem=send, recv_sem=recv, device_id=to, device_id_type=MESH
        )

    def z_up(r, c, src=None):
        dst = rows(c_all, c, r)
        return remote(dst if src is None else src, dst, up_send.at[r, c], z_recv.at[r, c], above)

    def z_down(r, c, src=None):
        dst = rows(c_all, c, r)
        return remote(dst if src is None else src, dst, down_send.at[r, c], z_recv.at[r, c], below)

    def to_across(inp, buf, c, send, recv):
        return remote(rows(inp, c), rows(buf, c, j), send.at[c], recv.at[c], across)

    def to_partner(inp, buf, c, send, recv):
        return remote(rows(inp, c), rows(buf, c, j), send.at[c], recv.at[c], partner)

    def forward(buf, c, send, recv):
        part = rows(buf, c, o)
        return remote(part, part, send.at[c], recv.at[c], partner)

    def row_to(c, core, src):
        return remote(
            src, rows(c_row, c, j), row_send.at[c], row_recv.at[u, c], (g, m, far, core)
        )

    def start_row(c, own):
        src = rows(c_in, c) if own else rows(c_all, c, sent_row)
        row_to(c, sent_row - 2 * far, src).start()

    def flow(b, c, to):
        part = rows(c_row, c, 2 * far + b)
        return remote(part, part, flow_send.at[b, c], row_recv.at[b, c], to)

    def cells_to_partner(c, src):
        return remote(src, rows(c_row, c, j), cp_send.at[c], cp_recv.at[c], partner)

    def got(buf, slot, c, recv):
        part = rows(buf, c, slot)
        remote(part, part, recv, recv, partner).wait_recv()

    barrier = pltpu.get_barrier_semaphore()
    for to in (partner, across, crossed):
        pl.semaphore_signal(barrier, inc=1, device_id=to, device_id_type=MESH)

    @pl.when(has_up)
    def _():
        pl.semaphore_signal(barrier, inc=1, device_id=above, device_id_type=MESH)

    @pl.when(has_down)
    def _():
        pl.semaphore_signal(barrier, inc=1, device_id=below, device_id_type=MESH)

    owns = (
        pltpu.make_async_copy(c_in, c_all.at[m], local_sem.at[0]),
        pltpu.make_async_copy(t_in, t_all.at[j], local_sem.at[1]),
        pltpu.make_async_copy(v_in, v_all.at[j], local_sem.at[2]),
    )
    for copy in owns:
        copy.start()
    pl.semaphore_wait(barrier, 3 + has_up.astype(jnp.int32) + has_down.astype(jnp.int32))

    for c in range(PIECES):

        @pl.when(has_up)
        def _():
            z_up(m, c, rows(c_in, c)).start()

        @pl.when(has_down)
        def _():
            z_down(m, c, rows(c_in, c)).start()

        @pl.when(sent_own)
        def _():
            start_row(c, True)

    for c in range(PIECES):
        to_across(t_in, t_all, c, tx_send, tx_recv).start()
    for c in range(PIECES):
        to_across(v_in, v_all, c, vx_send, vx_recv).start()
    for c in range(PIECES):
        to_partner(t_in, t_all, c, tp_send, tp_recv).start()
        to_partner(v_in, v_all, c, vp_send, vp_recv).start()

        @pl.when(m == p)
        def _():
            cells_to_partner(c, rows(c_in, c)).start()

    adj[...] = jnp.zeros_like(adj)
    grad[...] = jnp.zeros_like(grad)
    for copy in owns:
        copy.wait()

    def add_adj(k):
        @pl.loop(0, adj.shape[0] // TILE)
        def _(i):
            at = pl.ds(pl.multiple_of(i * TILE, TILE), TILE)
            adj[at, :] += lax.dot_general(
                t_all[k, :, at], c_all[k], (((0,), (0,)), ((), ())),
                preferred_element_type=jnp.float32,
            )

    def add_grad(buf, k_rows, k):
        @pl.loop(0, grad.shape[0] // TILE)
        def _(i):
            at = pl.ds(pl.multiple_of(i * TILE, TILE), TILE)
            grad[at, :] += lax.dot_general(
                buf[k_rows, at, :], v_all[k], (((1,), (1,)), ((), ())),
                preferred_element_type=jnp.float32,
            )

    def arrived(r, c):
        @pl.when(r == p)
        def _():
            cells_to_partner(c, rows(c_all, c, r)).start()

        @pl.when((r == sent_row) & jnp.logical_not(sent_own))
        def _():
            start_row(c, False)

    def z_step(d):
        for c in range(PIECES):

            @pl.when(m - d >= 0)
            def _():
                r = m - d
                got(c_all, r, c, z_recv.at[r, c])

                @pl.when(has_up)
                def _():
                    z_up(r, c).start()

                arrived(r, c)

            @pl.when(m + d <= n_z - 1)
            def _():
                r = m + d
                got(c_all, r, c, z_recv.at[r, c])

                @pl.when(has_down)
                def _():
                    z_down(r, c).start()

                arrived(r, c)

    def row_step(when):
        @pl.when(when)
        def _():
            for c in range(PIECES):
                for b in range(2):
                    got(c_row, 2 * far + b, c, row_recv.at[b, c])

                    @pl.when(flow_up)
                    def _():
                        flow(b, c, above).start()

                    @pl.when(flow_down)
                    def _():
                        flow(b, c, below).start()

    away = jnp.abs(m - j)

    def relay(buf, c, send, recv, x_recv):
        got(buf, o, c, x_recv.at[c])
        forward(buf, c, send, recv).start()

    z_step(1)
    row_step(away == 0)
    relay(t_all, 0, tf_send, tf_recv, tx_recv)
    z_step(2)
    row_step(jnp.logical_not(by_x) & (away == 1))
    relay(t_all, 1, tf_send, tf_recv, tx_recv)
    z_step(3)
    row_step(jnp.logical_not(by_x) & (away == 2))
    for c in range(PIECES):
        got(t_all, p, c, tp_recv.at[c])
    add_adj(j)
    add_adj(p)
    relay(v_all, 0, vf_send, vf_recv, vx_recv)
    for c in range(PIECES):
        got(v_all, p, c, vp_recv.at[c])
        got(c_row, p, c, cp_recv.at[c])
    add_grad(c_all, j, j)
    add_grad(c_row, p, p)
    relay(v_all, 1, vf_send, vf_recv, vx_recv)
    add_adj(o)
    for c in range(PIECES):
        got(t_all, q, c, tf_recv.at[c])
    add_adj(q)
    row_step((by_x & (away > 0)) | (jnp.logical_not(by_x) & (away == 3)))
    add_grad(c_row, o, o)
    for c in range(PIECES):
        got(v_all, q, c, vf_recv.at[c])
    add_grad(c_row, q, q)

    for c in range(PIECES):
        for r in range(n_z):

            @pl.when(has_up & (r <= m))
            def _():
                z_up(r, c).wait_send()

            @pl.when(has_down & (r >= m))
            def _():
                z_down(r, c).wait_send()

        row_to(c, u, rows(c_in, c)).wait_send()
        cells_to_partner(c, rows(c_in, c)).wait_send()
        to_across(t_in, t_all, c, tx_send, tx_recv).wait_send()
        to_across(v_in, v_all, c, vx_send, vx_recv).wait_send()
        to_partner(t_in, t_all, c, tp_send, tp_recv).wait_send()
        to_partner(v_in, v_all, c, vp_send, vp_recv).wait_send()
        forward(t_all, c, tf_send, tf_recv).wait_send()
        forward(v_all, c, vf_send, vf_recv).wait_send()
        for b in range(2):

            @pl.when(flow_up | flow_down)
            def _():
                flow(b, c, above).wait_send()


def exchanged(n_z, expected_cot, value_next, transition, section):
    states, cells = expected_cot.shape
    current, following = transition.shape
    dma = pltpu.SemaphoreType.DMA
    piece = dma((PIECES,))
    adjoint_sum, gradient_sum = pl.pallas_call(
        functools.partial(kernel, n_z),
        out_shape=(
            jax.ShapeDtypeStruct((following, cells), jnp.float32),
            jax.ShapeDtypeStruct((current, following), jnp.float32),
        ),
        in_specs=[pl.BlockSpec(memory_space=pl.ANY)] * 3,
        out_specs=(pl.BlockSpec(memory_space=pltpu.VMEM),) * 2,
        scratch_shapes=[
            pltpu.VMEM((n_z, states, cells), jnp.bfloat16),
            pltpu.VMEM((4, current, cells), jnp.bfloat16),
            pltpu.VMEM((4, current, following), jnp.bfloat16),
            pltpu.VMEM((4, states, cells), jnp.bfloat16),
            dma((3,)),
            dma((n_z, PIECES)),
            dma((n_z, PIECES)),
            dma((n_z, PIECES)),
            *([piece] * 14),
            piece,
            dma((2, PIECES)),
            dma((2, PIECES)),
        ],
        compiler_params=pltpu.CompilerParams(
            collective_id=0, has_side_effects=True, vmem_limit_bytes=48 * 1024 * 1024
        ),
    )(expected_cot, value_next, transition)
    discount_factor = discount_of(section)
    return (discount_factor * adjoint_sum, discount_factor * gradient_sum)


def solution(mesh):
    shape = mesh.shape
    paired = shape["storage"] == 2 and shape["sub"] == 2 and shape["markov"] == 4
    body = functools.partial(exchanged, shape["markov"]) if paired else gathered
    return jax.shard_map(
        body,
        mesh=mesh,
        in_specs=(
            P(("groups", "markov"), ("storage", "sub")),
            P(("groups", "markov"), ("storage", "sub")),
            P(("groups", "storage", "sub"), "markov"),
            P("groups"),
        ),
        out_specs=(
            P(("groups", "markov"), ("storage", "sub")),
            P(("groups", "storage", "sub"), "markov"),
        ),
        check_vma=False,
    )
```

```python
import functools

import jax
import jax.numpy as jnp
from jax import lax
from jax.experimental import pallas as pl
from jax.experimental.pallas import tpu as pltpu
from jax.sharding import PartitionSpec as P

discount_rate = 0.97
MESH = pl.DeviceIdType.MESH
PIECES = 2
TILE = 256
VMEM_BYTES = 34 * 1024 * 1024


def discount_of(section):
    return jnp.exp(section[0].astype(jnp.float32) * jnp.log(jnp.float32(discount_rate)))


def gathered(expected_cot, value_next, transition, section):
    discount_factor = discount_of(section)
    cotangent_all = lax.all_gather(expected_cot, "markov", axis=0, tiled=True)
    adjoint_sum = lax.dot_general(
        lax.all_gather(transition, ("storage", "sub"), axis=0, tiled=True),
        cotangent_all,
        (((0,), (0,)), ((), ())),
        preferred_element_type=jnp.float32,
    )
    own_states = lax.all_to_all(
        cotangent_all, ("storage", "sub"), split_axis=0, concat_axis=1, tiled=True
    )
    gathered_values = lax.all_gather(value_next, ("storage", "sub"), axis=1, tiled=True)
    gradient_sum = lax.dot_general(
        own_states, gathered_values, (((1,), (1,)), ((), ())), preferred_element_type=jnp.float32
    )
    return (discount_factor * adjoint_sum, discount_factor * gradient_sum)


def kernel(
    n_z, c_in, v_in, t_in, adj, grad, c_all, c_row, t_all, v_all,
    local_sem, z_recv, up_send, down_send, tx_send, tx_recv, vx_send, vx_recv,
    tf_send, tf_recv, vf_send, vf_recv, tp_send, tp_recv, vp_send, vp_recv,
    cp_send, cp_recv, row_send, row_recv, flow_send,
):
    g, m = lax.axis_index("groups"), lax.axis_index("markov")
    s, u = lax.axis_index("storage"), lax.axis_index("sub")
    far = 1 - s
    j, p = 2 * s + u, 2 * s + 1 - u
    o, q = 2 * far + u, 2 * far + 1 - u
    partner, across, crossed = (g, m, s, 1 - u), (g, m, far, u), (g, m, far, 1 - u)
    above, below = (g, lax.rem(m + 1, n_z), s, u), (g, lax.rem(m + n_z - 1, n_z), s, u)
    has_up, has_down = m < n_z - 1, m > 0

    def crossing_row(chip, z):
        return jnp.clip(z, 2 * chip, 2 * chip + 1)

    sent_row = crossing_row(far, m)
    sent_own = sent_row == m
    by_x = crossing_row(s, m) == j
    flow_up = (m >= j) & has_up & (crossing_row(s, m + 1) != j)
    flow_down = (m <= j) & has_down & (crossing_row(s, m - 1) != j)

    def rows(ref, piece, *lead):
        step = ref.shape[-2] // PIECES
        return ref.at[(*lead, pl.ds(piece * step, step))]

    def remote(src, dst, send, recv, to):
        return pltpu.make_async_remote_copy(
            src_ref=src, dst_ref=dst, send_sem=send, recv_sem=recv, device_id=to, device_id_type=MESH
        )

    def z_up(r, c, src=None):
        dst = rows(c_all, c, r)
        return remote(dst if src is None else src, dst, up_send.at[r, c], z_recv.at[r, c], above)

    def z_down(r, c, src=None):
        dst = rows(c_all, c, r)
        return remote(dst if src is None else src, dst, down_send.at[r, c], z_recv.at[r, c], below)

    def to_across(inp, buf, c, send, recv):
        return remote(rows(inp, c), rows(buf, c, j), send.at[c], recv.at[c], across)

    def to_partner(inp, buf, c, send, recv):
        return remote(rows(inp, c), rows(buf, c, j), send.at[c], recv.at[c], partner)

    def forward(buf, c, send, recv):
        part = rows(buf, c, o)
        return remote(part, part, send.at[c], recv.at[c], partner)

    def row_to(c, core, src):
        return remote(
            src, rows(c_row, c, j), row_send.at[c], row_recv.at[u, c], (g, m, far, core)
        )

    def start_row(c, own):
        src = rows(c_in, c) if own else rows(c_all, c, sent_row)
        row_to(c, sent_row - 2 * far, src).start()

    def flow(b, c, to):
        part = rows(c_row, c, 2 * far + b)
        return remote(part, part, flow_send.at[b, c], row_recv.at[b, c], to)

    def cells_to_partner(c, src):
        return remote(src, rows(c_row, c, j), cp_send.at[c], cp_recv.at[c], partner)

    def got(buf, slot, c, recv):
        part = rows(buf, c, slot)
        remote(part, part, recv, recv, partner).wait_recv()

    barrier = pltpu.get_barrier_semaphore()
    for to in (partner, across, crossed):
        pl.semaphore_signal(barrier, inc=1, device_id=to, device_id_type=MESH)

    @pl.when(has_up)
    def _():
        pl.semaphore_signal(barrier, inc=1, device_id=above, device_id_type=MESH)

    @pl.when(has_down)
    def _():
        pl.semaphore_signal(barrier, inc=1, device_id=below, device_id_type=MESH)

    owns = (
        pltpu.make_async_copy(c_in, c_all.at[m], local_sem.at[0]),
        pltpu.make_async_copy(t_in, t_all.at[j], local_sem.at[1]),
        pltpu.make_async_copy(v_in, v_all.at[j], local_sem.at[2]),
    )
    for copy in owns:
        copy.start()
    pl.semaphore_wait(barrier, 3 + has_up.astype(jnp.int32) + has_down.astype(jnp.int32))

    for c in range(PIECES):

        @pl.when(has_up)
        def _():
            z_up(m, c, rows(c_in, c)).start()

        @pl.when(has_down)
        def _():
            z_down(m, c, rows(c_in, c)).start()

        @pl.when(sent_own)
        def _():
            start_row(c, True)

    for c in range(PIECES):
        to_across(t_in, t_all, c, tx_send, tx_recv).start()
    for c in range(PIECES):
        to_across(v_in, v_all, c, vx_send, vx_recv).start()
    for c in range(PIECES):
        to_partner(t_in, t_all, c, tp_send, tp_recv).start()
        to_partner(v_in, v_all, c, vp_send, vp_recv).start()

        @pl.when(m == p)
        def _():
            cells_to_partner(c, rows(c_in, c)).start()

    adj[...] = jnp.zeros_like(adj)
    grad[...] = jnp.zeros_like(grad)

    def add_adj(k):
        @pl.loop(0, adj.shape[0] // TILE)
        def _(i):
            at = pl.ds(pl.multiple_of(i * TILE, TILE), TILE)
            adj[at, :] += lax.dot_general(
                t_all[k, :, at], c_all[k], (((0,), (0,)), ((), ())),
                preferred_element_type=jnp.float32,
            )

    def add_grad(buf, k, top=0, many=grad.shape[0], cut=pl.ds(0, grad.shape[1])):
        @pl.loop(0, many // TILE)
        def _(i):
            at = pl.ds(pl.multiple_of(top + i * TILE, TILE), TILE)
            grad[at, cut] += lax.dot_general(
                buf[k, at, :], v_all[k, cut, :], (((1,), (1,)), ((), ())),
                preferred_element_type=jnp.float32,
            )

    def arrived(r, c):
        @pl.when(r == p)
        def _():
            cells_to_partner(c, rows(c_all, c, r)).start()

        @pl.when((r == sent_row) & jnp.logical_not(sent_own))
        def _():
            start_row(c, False)

    def z_step(d, c):
        @pl.when(m - d >= 0)
        def _():
            r = m - d
            got(c_all, r, c, z_recv.at[r, c])

            @pl.when(has_up)
            def _():
                z_up(r, c).start()

            arrived(r, c)

        @pl.when(m + d <= n_z - 1)
        def _():
            r = m + d
            got(c_all, r, c, z_recv.at[r, c])

            @pl.when(has_down)
            def _():
                z_down(r, c).start()

            arrived(r, c)

    def row_step(c, when):
        @pl.when(when)
        def _():
            for b in range(2):
                got(c_row, 2 * far + b, c, row_recv.at[b, c])

                @pl.when(flow_up)
                def _():
                    flow(b, c, above).start()

                @pl.when(flow_down)
                def _():
                    flow(b, c, below).start()

    away, away_p = jnp.abs(m - j), jnp.abs(m - p)
    row_first = crossing_row(s, m) == m

    def relay(buf, c, send, recv, x_recv):
        got(buf, o, c, x_recv.at[c])
        forward(buf, c, send, recv).start()

    def partner_blocks():
        for c in range(PIECES):
            got(t_all, p, c, tp_recv.at[c])
            got(v_all, p, c, vp_recv.at[c])

    def near(d):
        @pl.when(away == d)
        def _():
            add_adj(j)
            add_grad(c_all, j)

        @pl.when(away_p == d)
        def _():
            add_adj(p)

    def partner_cells():
        for c in range(PIECES):
            got(c_row, p, c, cp_recv.at[c])
        add_grad(c_row, p)

    def far_adj():
        add_adj(o)
        for c in range(PIECES):
            got(t_all, q, c, tf_recv.at[c])
        add_adj(q)

    def cut_of(c):
        wide = grad.shape[1] // PIECES
        return pl.ds(c * wide, wide)

    def grad_by_values(c):
        @pl.when(row_first)
        def _():
            relay(v_all, c, vf_send, vf_recv, vx_recv)
            add_grad(c_row, o, cut=cut_of(c))
            got(v_all, q, c, vf_recv.at[c])
            add_grad(c_row, q, cut=cut_of(c))

    def values_early(c):
        @pl.when(jnp.logical_not(row_first))
        def _():
            relay(v_all, c, vf_send, vf_recv, vx_recv)
            got(v_all, q, c, vf_recv.at[c])

    def grad_by_rows(c):
        tall = grad.shape[0] // PIECES

        @pl.when(jnp.logical_not(row_first))
        def _():
            add_grad(c_row, o, c * tall, tall)
            add_grad(c_row, q, c * tall, tall)

    tasks = []
    block = 22.0
    for c in range(PIECES):
        part = block * (c + 1) / PIECES
        for d in range(1, n_z):
            tasks.append((block * (d - 1) + part, functools.partial(z_step, d, c)))
        tasks.append((part + 0.1, functools.partial(row_step, c, away == 0)))
        for h in range(1, n_z):
            when = jnp.logical_not(by_x) & (away == h)
            tasks.append((block * h + part + 0.2, functools.partial(row_step, c, when)))
        late = by_x & (away > 0)
        tasks.append((3 * block + part + 0.3, functools.partial(row_step, c, late)))
        tasks.append(
            (
                block + 2 * part,
                functools.partial(relay, t_all, c, tf_send, tf_recv, tx_recv),
            )
        )
        tasks.append((2 * block + part + 4, functools.partial(values_early, c)))
        tasks.append((3 * block + part + 1, functools.partial(grad_by_values, c)))
        tasks.append((3 * block + part + 1.1, functools.partial(grad_by_rows, c)))
    tasks.append((5.0, partner_blocks))
    for d in range(n_z):
        tasks.append((block * d + 0.5 + 5.0 * (d == 0), functools.partial(near, d)))
    tasks.append((3 * block + 0.7, partner_cells))
    tasks.append((3 * block + 3, far_adj))
    for copy in owns:
        copy.wait()
    for _, task in sorted(tasks, key=lambda entry: entry[0]):
        task()

    for c in range(PIECES):
        for r in range(n_z):

            @pl.when(has_up & (r <= m))
            def _():
                z_up(r, c).wait_send()

            @pl.when(has_down & (r >= m))
            def _():
                z_down(r, c).wait_send()

        row_to(c, u, rows(c_in, c)).wait_send()
        cells_to_partner(c, rows(c_in, c)).wait_send()
        to_across(t_in, t_all, c, tx_send, tx_recv).wait_send()
        to_across(v_in, v_all, c, vx_send, vx_recv).wait_send()
        to_partner(t_in, t_all, c, tp_send, tp_recv).wait_send()
        to_partner(v_in, v_all, c, vp_send, vp_recv).wait_send()
        forward(t_all, c, tf_send, tf_recv).wait_send()
        forward(v_all, c, vf_send, vf_recv).wait_send()
        for b in range(2):

            @pl.when(flow_up | flow_down)
            def _():
                flow(b, c, above).wait_send()


def exchanged(n_z, expected_cot, value_next, transition, section):
    states, cells = expected_cot.shape
    current, following = transition.shape
    dma = pltpu.SemaphoreType.DMA
    piece = dma((PIECES,))
    adjoint_sum, gradient_sum = pl.pallas_call(
        functools.partial(kernel, n_z),
        out_shape=(
            jax.ShapeDtypeStruct((following, cells), jnp.float32),
            jax.ShapeDtypeStruct((current, following), jnp.float32),
        ),
        in_specs=[pl.BlockSpec(memory_space=pltpu.HBM)] * 3,
        out_specs=(pl.BlockSpec(memory_space=pltpu.VMEM),) * 2,
        scratch_shapes=[
            pltpu.VMEM((n_z, states, cells), jnp.bfloat16),
            pltpu.VMEM((4, current, cells), jnp.bfloat16),
            pltpu.VMEM((4, current, following), jnp.bfloat16),
            pltpu.VMEM((4, states, cells), jnp.bfloat16),
            dma((3,)),
            dma((n_z, PIECES)),
            dma((n_z, PIECES)),
            dma((n_z, PIECES)),
            *([piece] * 14),
            piece,
            dma((2, PIECES)),
            dma((2, PIECES)),
        ],
        compiler_params=pltpu.CompilerParams(
            collective_id=0, has_side_effects=True, vmem_limit_bytes=VMEM_BYTES
        ),
    )(expected_cot, value_next, transition)
    discount_factor = discount_of(section)
    return (discount_factor * adjoint_sum, discount_factor * gradient_sum)


def solution(mesh):
    shape = mesh.shape
    paired = shape["storage"] == 2 and shape["sub"] == 2 and shape["markov"] == 4
    body = functools.partial(exchanged, shape["markov"]) if paired else gathered
    return jax.shard_map(
        body,
        mesh=mesh,
        in_specs=(
            P(("groups", "markov"), ("storage", "sub")),
            P(("groups", "markov"), ("storage", "sub")),
            P(("groups", "storage", "sub"), "markov"),
            P("groups"),
        ),
        out_specs=(
            P(("groups", "markov"), ("storage", "sub")),
            P(("groups", "storage", "sub"), "markov"),
        ),
        check_vma=False,
    )
```

```python
import functools

import jax
import jax.numpy as jnp
from jax import lax
from jax.experimental import pallas as pl
from jax.experimental.pallas import tpu as pltpu
from jax.sharding import PartitionSpec as P

discount_rate = 0.97
MESH = pl.DeviceIdType.MESH
PIECES = 2
TILE = 256
VMEM_BYTES = 34 * 1024 * 1024


def discount_of(section):
    return jnp.exp(section[0].astype(jnp.float32) * jnp.log(jnp.float32(discount_rate)))


def gathered(expected_cot, value_next, transition, section):
    discount_factor = discount_of(section)
    cotangent_all = lax.all_gather(expected_cot, "markov", axis=0, tiled=True)
    adjoint_sum = lax.dot_general(
        lax.all_gather(transition, ("storage", "sub"), axis=0, tiled=True),
        cotangent_all,
        (((0,), (0,)), ((), ())),
        preferred_element_type=jnp.float32,
    )
    own_states = lax.all_to_all(
        cotangent_all, ("storage", "sub"), split_axis=0, concat_axis=1, tiled=True
    )
    gathered_values = lax.all_gather(value_next, ("storage", "sub"), axis=1, tiled=True)
    gradient_sum = lax.dot_general(
        own_states, gathered_values, (((1,), (1,)), ((), ())), preferred_element_type=jnp.float32
    )
    return (discount_factor * adjoint_sum, discount_factor * gradient_sum)


def kernel(
    n_z, c_in, v_in, t_in, adj, grad, c_all, c_row, t_all, v_all,
    local_sem, z_recv, up_send, down_send, tx_send, tx_recv, vx_send, vx_recv,
    tf_send, tf_recv, vf_send, vf_recv, tp_send, tp_recv, vp_send, vp_recv,
    cp_send, cp_recv, row_send, row_recv, flow_send,
):
    g, m = lax.axis_index("groups"), lax.axis_index("markov")
    s, u = lax.axis_index("storage"), lax.axis_index("sub")
    far = 1 - s
    j, p = 2 * s + u, 2 * s + 1 - u
    o, q = 2 * far + u, 2 * far + 1 - u
    partner, across, crossed = (g, m, s, 1 - u), (g, m, far, u), (g, m, far, 1 - u)
    above, below = (g, lax.rem(m + 1, n_z), s, u), (g, lax.rem(m + n_z - 1, n_z), s, u)
    has_up, has_down = m < n_z - 1, m > 0

    def crossing_row(chip, z):
        return jnp.clip(z, 2 * chip, 2 * chip + 1)

    sent_row = crossing_row(far, m)
    sent_own = sent_row == m
    by_x = crossing_row(s, m) == j
    flow_up = (m >= j) & has_up & (crossing_row(s, m + 1) != j)
    flow_down = (m <= j) & has_down & (crossing_row(s, m - 1) != j)

    def rows(ref, piece, *lead):
        step = ref.shape[-2] // PIECES
        return ref.at[(*lead, pl.ds(piece * step, step))]

    def remote(src, dst, send, recv, to):
        return pltpu.make_async_remote_copy(
            src_ref=src, dst_ref=dst, send_sem=send, recv_sem=recv, device_id=to, device_id_type=MESH
        )

    def z_up(r, c, src=None):
        dst = rows(c_all, c, r)
        return remote(dst if src is None else src, dst, up_send.at[r, c], z_recv.at[r, c], above)

    def z_down(r, c, src=None):
        dst = rows(c_all, c, r)
        return remote(dst if src is None else src, dst, down_send.at[r, c], z_recv.at[r, c], below)

    def to_across(inp, buf, c, send, recv):
        return remote(rows(inp, c), rows(buf, c, j), send.at[c], recv.at[c], across)

    def to_partner(inp, buf, c, send, recv):
        return remote(rows(inp, c), rows(buf, c, j), send.at[c], recv.at[c], partner)

    def forward(buf, c, send, recv):
        part = rows(buf, c, o)
        return remote(part, part, send.at[c], recv.at[c], partner)

    def row_to(c, core, src):
        return remote(
            src, rows(c_row, c, j), row_send.at[c], row_recv.at[u, c], (g, m, far, core)
        )

    def start_row(c, own):
        src = rows(c_in, c) if own else rows(c_all, c, sent_row)
        row_to(c, sent_row - 2 * far, src).start()

    def flow(b, c, to):
        part = rows(c_row, c, 2 * far + b)
        return remote(part, part, flow_send.at[b, c], row_recv.at[b, c], to)

    def cells_to_partner(c, src):
        return remote(src, rows(c_row, c, j), cp_send.at[c], cp_recv.at[c], partner)

    def got(buf, slot, c, recv):
        part = rows(buf, c, slot)
        remote(part, part, recv, recv, partner).wait_recv()

    barrier = pltpu.get_barrier_semaphore()
    for to in (partner, across, crossed):
        pl.semaphore_signal(barrier, inc=1, device_id=to, device_id_type=MESH)

    @pl.when(has_up)
    def _():
        pl.semaphore_signal(barrier, inc=1, device_id=above, device_id_type=MESH)

    @pl.when(has_down)
    def _():
        pl.semaphore_signal(barrier, inc=1, device_id=below, device_id_type=MESH)

    owns = (
        pltpu.make_async_copy(c_in, c_all.at[m], local_sem.at[0]),
        pltpu.make_async_copy(t_in, t_all.at[j], local_sem.at[1]),
        pltpu.make_async_copy(v_in, v_all.at[j], local_sem.at[2]),
    )
    for copy in owns:
        copy.start()
    pl.semaphore_wait(barrier, 3 + has_up.astype(jnp.int32) + has_down.astype(jnp.int32))

    for c in range(PIECES):

        @pl.when(has_up)
        def _():
            z_up(m, c, rows(c_in, c)).start()

        @pl.when(has_down)
        def _():
            z_down(m, c, rows(c_in, c)).start()

        @pl.when(sent_own)
        def _():
            start_row(c, True)

    for c in range(PIECES):
        to_across(t_in, t_all, c, tx_send, tx_recv).start()
    for c in range(PIECES):
        to_across(v_in, v_all, c, vx_send, vx_recv).start()
    for c in range(PIECES):
        to_partner(t_in, t_all, c, tp_send, tp_recv).start()
        to_partner(v_in, v_all, c, vp_send, vp_recv).start()

        @pl.when(m == p)
        def _():
            cells_to_partner(c, rows(c_in, c)).start()

    adj[...] = jnp.zeros_like(adj)
    grad[...] = jnp.zeros_like(grad)

    def add_adj(k):
        @pl.loop(0, adj.shape[0] // TILE)
        def _(i):
            at = pl.ds(pl.multiple_of(i * TILE, TILE), TILE)
            adj[at, :] += lax.dot_general(
                t_all[k, :, at], c_all[k], (((0,), (0,)), ((), ())),
                preferred_element_type=jnp.float32,
            )

    def add_grad(buf, k, top=0, many=grad.shape[0], cut=pl.ds(0, grad.shape[1])):
        @pl.loop(0, many // TILE)
        def _(i):
            at = pl.ds(pl.multiple_of(top + i * TILE, TILE), TILE)
            grad[at, cut] += lax.dot_general(
                buf[k, at, :], v_all[k, cut, :], (((1,), (1,)), ((), ())),
                preferred_element_type=jnp.float32,
            )

    def arrived(r, c):
        @pl.when(r == p)
        def _():
            cells_to_partner(c, rows(c_all, c, r)).start()

        @pl.when((r == sent_row) & jnp.logical_not(sent_own))
        def _():
            start_row(c, False)

    def z_step(d, c):
        @pl.when(m - d >= 0)
        def _():
            r = m - d
            got(c_all, r, c, z_recv.at[r, c])

            @pl.when(has_up)
            def _():
                z_up(r, c).start()

            arrived(r, c)

        @pl.when(m + d <= n_z - 1)
        def _():
            r = m + d
            got(c_all, r, c, z_recv.at[r, c])

            @pl.when(has_down)
            def _():
                z_down(r, c).start()

            arrived(r, c)

    def flow_on(c, when):
        @pl.when(when & flow_up)
        def _():
            for b in range(2):
                flow(b, c, above).start()

        @pl.when(when & flow_down)
        def _():
            for b in range(2):
                flow(b, c, below).start()

    def row_step(c, when):
        @pl.when(when)
        def _():
            for b in range(2):
                got(c_row, 2 * far + b, c, row_recv.at[b, c])

            flow_on(c, jnp.logical_not(one_hop))

    away, away_p = jnp.abs(m - j), jnp.abs(m - p)
    row_first = crossing_row(s, m) == m
    one_hop = (j == 1) | (j == 2)
    rows_late = one_hop & jnp.logical_not(by_x) & (away == 1)

    def relay(buf, c, send, recv, x_recv):
        got(buf, o, c, x_recv.at[c])
        forward(buf, c, send, recv).start()

    def partner_blocks():
        for c in range(PIECES):
            got(t_all, p, c, tp_recv.at[c])
            got(v_all, p, c, vp_recv.at[c])

    def near(d):
        @pl.when(away == d)
        def _():
            add_adj(j)
            add_grad(c_all, j)

        @pl.when(away_p == d)
        def _():
            add_adj(p)

    def partner_cells():
        for c in range(PIECES):
            got(c_row, p, c, cp_recv.at[c])
        add_grad(c_row, p)

    def far_adj():
        add_adj(o)
        for c in range(PIECES):
            got(t_all, q, c, tf_recv.at[c])
        add_adj(q)

    def cut_of(c):
        wide = grad.shape[1] // PIECES
        return pl.ds(c * wide, wide)

    def grad_by_values(c):
        @pl.when(row_first)
        def _():
            relay(v_all, c, vf_send, vf_recv, vx_recv)

            @pl.when(jnp.logical_not(rows_late))
            def _():
                add_grad(c_row, o, cut=cut_of(c))
                got(v_all, q, c, vf_recv.at[c])
                add_grad(c_row, q, cut=cut_of(c))

            @pl.when(rows_late)
            def _():
                for b in range(2):
                    got(c_row, 2 * far + b, c, row_recv.at[b, c])
                tall = grad.shape[0] // PIECES
                for k in (o, q):
                    if c:
                        add_grad(c_row, k, c * tall, tall, pl.ds(0, cut_of(c).start))
                    if k is q:
                        got(v_all, q, c, vf_recv.at[c])
                    add_grad(c_row, k, 0, (c + 1) * tall, cut_of(c))

    def values_early(c):
        @pl.when(jnp.logical_not(row_first))
        def _():
            relay(v_all, c, vf_send, vf_recv, vx_recv)
            got(v_all, q, c, vf_recv.at[c])

    def grad_by_rows(c):
        tall = grad.shape[0] // PIECES

        @pl.when(jnp.logical_not(row_first))
        def _():
            add_grad(c_row, o, c * tall, tall)
            add_grad(c_row, q, c * tall, tall)

    tasks = []
    block = 22.0
    for c in range(PIECES):
        part = block * (c + 1) / PIECES
        for d in range(1, n_z):
            tasks.append((block * (d - 1) + part, functools.partial(z_step, d, c)))
        tasks.append((part + 0.1, functools.partial(row_step, c, away == 0)))
        for h in range(1, n_z):
            when = jnp.logical_not(by_x | rows_late) & (away == h)
            tasks.append((block * h + part + 0.2, functools.partial(row_step, c, when)))
        tasks.append((block + part + 0.15, functools.partial(flow_on, c, one_hop & (away == 0))))
        late = by_x & (away > 0)
        tasks.append((3 * block + part + 0.3, functools.partial(row_step, c, late)))
        tasks.append(
            (
                block + 2 * part,
                functools.partial(relay, t_all, c, tf_send, tf_recv, tx_recv),
            )
        )
        tasks.append((2 * block + part + 4, functools.partial(values_early, c)))
        tasks.append((3 * block + part + 1, functools.partial(grad_by_values, c)))
        tasks.append((3 * block + part + 1.1, functools.partial(grad_by_rows, c)))
    tasks.append((5.0, partner_blocks))
    for d in range(n_z):
        tasks.append((block * d + 0.5 + 5.0 * (d == 0), functools.partial(near, d)))
    tasks.append((3 * block + 0.7, partner_cells))
    tasks.append((3 * block + 3, far_adj))
    for copy in owns:
        copy.wait()
    for _, task in sorted(tasks, key=lambda entry: entry[0]):
        task()

    for c in range(PIECES):
        for r in range(n_z):

            @pl.when(has_up & (r <= m))
            def _():
                z_up(r, c).wait_send()

            @pl.when(has_down & (r >= m))
            def _():
                z_down(r, c).wait_send()

        row_to(c, u, rows(c_in, c)).wait_send()
        cells_to_partner(c, rows(c_in, c)).wait_send()
        to_across(t_in, t_all, c, tx_send, tx_recv).wait_send()
        to_across(v_in, v_all, c, vx_send, vx_recv).wait_send()
        to_partner(t_in, t_all, c, tp_send, tp_recv).wait_send()
        to_partner(v_in, v_all, c, vp_send, vp_recv).wait_send()
        forward(t_all, c, tf_send, tf_recv).wait_send()
        forward(v_all, c, vf_send, vf_recv).wait_send()
        for b in range(2):

            @pl.when(flow_up | flow_down)
            def _():
                flow(b, c, above).wait_send()


def exchanged(n_z, expected_cot, value_next, transition, section):
    states, cells = expected_cot.shape
    current, following = transition.shape
    dma = pltpu.SemaphoreType.DMA
    piece = dma((PIECES,))
    adjoint_sum, gradient_sum = pl.pallas_call(
        functools.partial(kernel, n_z),
        out_shape=(
            jax.ShapeDtypeStruct((following, cells), jnp.float32),
            jax.ShapeDtypeStruct((current, following), jnp.float32),
        ),
        in_specs=[pl.BlockSpec(memory_space=pltpu.HBM)] * 3,
        out_specs=(pl.BlockSpec(memory_space=pltpu.VMEM),) * 2,
        scratch_shapes=[
            pltpu.VMEM((n_z, states, cells), jnp.bfloat16),
            pltpu.VMEM((4, current, cells), jnp.bfloat16),
            pltpu.VMEM((4, current, following), jnp.bfloat16),
            pltpu.VMEM((4, states, cells), jnp.bfloat16),
            dma((3,)),
            dma((n_z, PIECES)),
            dma((n_z, PIECES)),
            dma((n_z, PIECES)),
            *([piece] * 14),
            piece,
            dma((2, PIECES)),
            dma((2, PIECES)),
        ],
        compiler_params=pltpu.CompilerParams(
            collective_id=0, has_side_effects=True, vmem_limit_bytes=VMEM_BYTES
        ),
    )(*(pltpu.with_memory_space_constraint(x, pltpu.HBM) for x in (expected_cot, value_next, transition)))
    discount_factor = discount_of(section)
    return (discount_factor * adjoint_sum, discount_factor * gradient_sum)


def solution(mesh):
    shape = mesh.shape
    paired = shape["storage"] == 2 and shape["sub"] == 2 and shape["markov"] == 4
    body = functools.partial(exchanged, shape["markov"]) if paired else gathered
    return jax.shard_map(
        body,
        mesh=mesh,
        in_specs=(
            P(("groups", "markov"), ("storage", "sub")),
            P(("groups", "markov"), ("storage", "sub")),
            P(("groups", "storage", "sub"), "markov"),
            P("groups"),
        ),
        out_specs=(
            P(("groups", "markov"), ("storage", "sub")),
            P(("groups", "storage", "sub"), "markov"),
        ),
        check_vma=False,
    )
```
